32 devices in a mesh: groups: 2 (over x), expert: 16 (over z, y, core).
Axes of the slice: x: 2, y: 2, z: 4, core: 2. Of those that a mesh axis runs over, the one named last changes fastest.
Arguments:
- hidden_states: bfloat16 [2, 1024, 2560], P(None, ('groups', 'expert')), parts along dimension 1, may hold values from -6 to 6
- route_ids: int32 [2, 1024, 8], P(None, ('groups', 'expert')), parts along dimension 1, may hold values from 0 to 15, all different within a row; in each aligned block of 32 rows (0 to 31, 32 to 63, ..., all dimensions but the last counted through in order) at most 24 rows name the same one
- route_weights: float32 [2, 1024, 8], P(None, ('groups', 'expert')), parts along dimension 1, may hold values from 0.05 to 1
- gate_proj: bfloat16 [16, 2560, 768], P('expert'), may hold values from -0.125 to 0.125
- up_proj: bfloat16 [16, 2560, 768], P('expert'), may hold values from -0.125 to 0.125
- down_proj: bfloat16 [16, 768, 2560], P('expert'), may hold values from -0.21875 to 0.21875
Outputs:
- moe_output: bfloat16 [2, 1024, 2560], P(None, ('groups', 'expert')), parts along dimension 1
The draws below stay inside these ranges and needn't reach their ends.
There are 2 independent parts, one for each index of `groups`. The reference program is written for one: setup_inputs(seed, part) draws one part's arguments, and reference() takes and returns one part's arrays. A program takes and returns all parts, laid end to end along the dimension named above; an argument that names none is the same for every part. Nothing has to cross between parts.
Inputs may be any that keep to these rules, and one draw needn't show every extreme that they name: `route_ids`: each row names 8 different experts. In each micro-batch, the 32 rows of one device name one expert at most 24 times, and some device names some expert exactly 24 times.
All inputs are finite; a program needn't handle non-finite values.
Results may differ from the reference program's by a relative error of at most 0.0057.
Values may be sent and summed in bfloat16 or wider, within the bound.
A program may use at most 64 MiB of HBM per device.

```python
import math
import jax
import jax.numpy as jnp
import numpy as np
from jax import lax

D = 2560
FF = 768
TOPK = 8
STEPS = 2
ROWS = 32
EXPERTS = 16
TOKENS = 512
CAP = 24
N_EXPERT = 16


def level_of(own_key, dims, cuts, smallest, largest):
    def one(dim, parts):
        heights = jax.random.uniform(jax.random.fold_in(jax.random.fold_in(own_key, 6), dim), (parts,), jnp.float32, smallest / len(cuts), largest / len(cuts))
        return jnp.repeat(jnp.exp(heights), dims[dim] // parts).reshape((-1,) + (1,) * (len(dims) - dim - 1))

    factor_of = one(*cuts[0])
    for cut in cuts[1:]:
        factor_of = factor_of * one(*cut)
    return factor_of


def routed_block(key, own, number, rows, amount, top, limit, lean):
    sequence = jax.random.permutation(key, amount)
    packed, ordinary = shares(amount, rows * top, limit, lean, True), shares(amount, rows * top, limit, lean, False)
    places = jnp.arange(amount)

    def named(tallies, offset_by):
        used = int((tallies > 0).sum())
        fixed = max(1, used // 4)
        shifted = fixed + (places - fixed + offset_by * (used - fixed)) % max(1, amount - fixed)
        return jnp.zeros((amount,), jnp.int32).at[sequence[jnp.where(places < fixed, places, shifted)]].set(jnp.asarray(tallies, jnp.int32))

    tallies = jnp.where(number % 4 == 0, named(packed, number // 4), named(ordinary, number - number // 4 - 1))
    mixed = jax.random.permutation(jax.random.fold_in(own, 3), amount)
    donor, receiver = mixed[0:amount // 2 * 2:2], mixed[1:amount // 2 * 2:2]
    room = jnp.minimum(tallies[donor] - 1, limit - tallies[receiver]) // 2
    room = jnp.where((donor == sequence[0]) | (receiver == sequence[0]) | (tallies[receiver] == 0), 0, jnp.maximum(room, 0))
    shifted = jax.random.randint(jax.random.fold_in(own, 4), (amount // 2,), 0, 1 << 20) % (room + 1)
    tallies = tallies.at[donor].add(-shifted).at[receiver].add(shifted)
    items = jnp.searchsorted(jnp.cumsum(tallies), jnp.arange(rows * top), side="right").astype(jnp.int32)
    table = items.reshape(top, rows).T
    table = table[jax.random.permutation(jax.random.fold_in(own, 1), rows)]
    offset_by = jax.random.randint(jax.random.fold_in(own, 2), (rows, 1), 0, top)
    return jnp.take_along_axis(table, (jnp.arange(top)[None, :] + offset_by) % top, axis=1)


def shares(number_of, total, limit, skew, full):
    portions = [(1 << 20) // math.isqrt(standing ** skew) + 1 for standing in range(1, number_of + 1)]
    largest = limit if full else min(limit, max(-(-total // number_of), total * portions[0] // sum(portions)))
    least = 1 if total - largest >= number_of - 1 else 0
    given, rest = [largest] + [least] * (number_of - 1), total - largest - least * (number_of - 1)
    while rest > 0:
        candidates = [i for i in range(1, number_of) if given[i] < largest] or [i for i in range(1, number_of) if given[i] < limit]
        pool, left = sum([portions[i] for i in candidates]), rest
        for i in candidates:
            extra = min(limit - given[i], max(1, left * portions[i] // pool), rest)
            given[i] = given[i] + extra
            rest = rest - extra
    return np.array(given)


def scatter_about(rng, extent, deviation, most, split=(), dtype=jnp.bfloat16):
    entries = deviation * jax.random.normal(rng, extent, jnp.float32)
    if split:
        entries = entries * level_of(rng, extent, split, -0.22, 0.18)
    return jnp.clip(entries, -most, most).astype(dtype)


def setup_inputs(seed: int = 0, part: int = 0) -> dict:
    keys = jax.random.split(jax.random.key(seed), 7)
    part_keys = jax.random.split(jax.random.fold_in(keys[6], part), 7)
    hidden_states = scatter_about(part_keys[0], (STEPS, TOKENS, D), 1.0, 6.0, ((1, 16),))
    route_ids_keys = jax.random.split(jax.random.fold_in(part_keys[1], 1), STEPS * TOKENS // ROWS)
    route_ids_turns = jax.random.permutation(jax.random.fold_in(part_keys[1], 3), STEPS * TOKENS // ROWS)
    route_ids = jax.vmap(lambda own, number: routed_block(jax.random.fold_in(part_keys[1], 2), own, number, ROWS, EXPERTS, TOPK, CAP, 2))(route_ids_keys, route_ids_turns).reshape((STEPS, TOKENS, TOPK))
    route_weights = jnp.clip(0.05 + 0.95 * jax.random.uniform(part_keys[2], (STEPS, TOKENS, TOPK), jnp.float32) ** level_of(part_keys[2], (STEPS, TOKENS, TOPK), ((1, 16),), -0.2, 0.2), 0.05, 1.0)
    gate_proj = scatter_about(keys[3], (EXPERTS, D, FF), D ** -0.5, 0.125, ((0, 16),))
    up_proj = scatter_about(keys[4], (EXPERTS, D, FF), D ** -0.5, 0.125, ((0, 16),))
    down_proj = scatter_about(keys[5], (EXPERTS, FF, D), FF ** -0.5, 0.21875, ((0, 16),))
    return dict(hidden_states=hidden_states, route_ids=route_ids, route_weights=route_weights, gate_proj=gate_proj, up_proj=up_proj, down_proj=down_proj)


def slot_targets(route_row, capacity):
    labels = lax.broadcasted_iota(jnp.int32, (TOKENS, TOPK, EXPERTS), 2)
    onehot = (route_row[:, :, None] == labels).astype(jnp.int32)
    per_row = jnp.sum(onehot, axis=1)
    before = jnp.cumsum(per_row, axis=0) - per_row
    position = jnp.sum(onehot * before[:, None, :], axis=2)
    return (route_row * capacity + position).astype(jnp.int32)


def apply_expert(operands):
    expert_rows, gate_weight, up_weight, down_weight = operands
    gate_values = jnp.dot(expert_rows, gate_weight, preferred_element_type=jnp.float32)
    up_values = jnp.dot(expert_rows, up_weight, preferred_element_type=jnp.float32)
    hidden = (jax.nn.silu(gate_values) * up_values).astype(jnp.bfloat16)
    return jnp.dot(hidden, down_weight, preferred_element_type=jnp.float32).astype(jnp.bfloat16)


def reference(hidden_states, route_ids, route_weights, gate_proj, up_proj, down_proj):
    capacity = N_EXPERT * CAP
    outputs = []
    for step_index in range(STEPS):
        targets = slot_targets(route_ids[step_index], capacity).reshape(-1)
        sources = jnp.repeat(hidden_states[step_index], TOPK, axis=0)
        buffer = jnp.zeros((EXPERTS * capacity, D), jnp.bfloat16).at[targets].set(sources)
        results = lax.map(apply_expert, (buffer.reshape(EXPERTS, capacity, D), gate_proj, up_proj, down_proj))
        gathered = results.reshape(EXPERTS * capacity, D)[targets].reshape(TOKENS, TOPK, D)
        weights = route_weights[step_index]
        normalized = weights / jnp.sum(weights, axis=1, keepdims=True)
        combined = jnp.sum(gathered.astype(jnp.float32) * normalized[:, :, None], axis=1)
        outputs.append(combined.astype(jnp.bfloat16))
    return jnp.stack(outputs)
```

```python
import functools
import itertools

import jax
import jax.numpy as jnp
from jax import lax
from jax.experimental import pallas as pl
from jax.experimental.pallas import tpu as pltpu
from jax.sharding import PartitionSpec as P

MESH = pl.DeviceIdType.MESH
LANES = 128
SIDES = 2
DOWNS = 5
PARTS = 2
HOP_US = 2.7
CHUNK_US = 0.9
PAIR_US = 1.5
BACK_US = 2.0
GATHER_US = 0.05
SUM_US = 0.15
GATE_UP_US = 0.5
DOWN_US = 0.4


import itertools, random
def reach(chips,d,q,S=2): return chips//2 if q//S==d else chips-1-chips//2
def slot_at(chips,d,hop): return hop if d==0 else (chips-hop)%chips
def slots_in_order(chips):
    order=[0]
    for hop in range(1,chips//2+1): order+=[s for s in dict.fromkeys((hop,chips-hop))]
    return order
DEF=dict(HOP=2.7,CHUNK=0.9,PAIR=1.5,BACK=2.0,AG=0.05,SUM=0.12,GU=0.34,DN=0.17,DOWNS=5,tiles=6,
         inj=0.2,inj_after=0,hold=0,rs_first=0,mm_gap=0.0,rs0_bias=0.0,S=2)
def plan(chips=8,steps=2,**kw):
    p=dict(DEF);p.update(kw); S=p['S']
    tiles=p['tiles'];D=p['DOWNS']
    order=slots_in_order(chips);per=chips//2
    part_of={s:i//per for i,s in enumerate(order)}
    chunks=range(2*S);ops=[];free=[0.,0.];due={};held={};now=0.
    busy=0.
    def send(key,d):
        start=max(now,free[d]);free[d]=start+p['CHUNK'];due[key]=free[d]+p['HOP']
    later=[(st,d,q) for st in range(1,steps) for q in chunks for d in range(2)]
    for q in chunks:
        for d in range(2):
            ops.append(("own",0,d,q));send(("ag",0,d,1,q),d)
    for st in range(steps):
        for q in chunks: held[st,0,q]=0.
    mm=[(st,pt,pc) for st in range(steps) for pt in range(2) for pc in range(tiles+S*D)]
    scaled={}
    wrs=[(st,d,h,q) for st in range(steps) for q in chunks for d in range(2) for h in range(reach(chips,d,q,S),0,-1)]
    wc=[(st,q) for st in range(steps) for q in chunks]
    agleft={st:sum(reach(chips,d,q,S)-1 for q in chunks for d in range(2)) for st in range(steps)}
    def part_time(st,part):
        last=0.
        for s in order[part*per:(part+1)*per]:
            for q in chunks:
                for key,ex in (((st,s,q),0.),((st,(chips-s)%chips,q),p['PAIR'])):
                    if key not in held: return None
                    last=max(last,held[key]+ex)
        return last
    def summed(st,s,q):
        a=(st,part_of[s],q%S);b=(st,part_of[(chips-s)%chips],q%S)
        if a not in scaled or b not in scaled: return None
        return max(scaled[a],scaled[b]+p['BACK'])
    while mm or wrs or wc or due:
        if agleft[0]<=p['inj_after']:
            for e in list(later):
                st,d,q=e
                if free[d]<=now+p['inj'] and not any(f[1]==d for f in later[:later.index(e)]):
                    later.remove(e);ops.append(("own",st,d,q));send(("ag",st,d,1,q),d)
        ready=[]
        for key,when in due.items():
            if key[0]=="ag": ready.append((when,key))
        for st,d,h,q in wrs:
            when=summed(st,slot_at(chips,d,h),q)
            if when is None: continue
            if h<reach(chips,d,q,S):
                if ("rs",st,d,h+1,q) not in due: continue
                when=max(when,due["rs",st,d,h+1,q])
            ready.append((when,("sum",st,d,h,q)))
        for st,q in wc:
            when=summed(st,0,q)
            if when is None or any(("rs",st,d,1,q) not in due for d in range(2)): continue
            ready.append((max([when]+[due["rs",st,d,1,q] for d in range(2)]),("close",st,q)))
        def prio(e):
            when,k=e
            cls={"ag":0,"sum":1 if not p['rs_first'] else -1,"close":5}[k[0]]
            if k[0]=="ag" and k[1]==1: cls+=0.5
            return (max(when,now),k[1],cls,when,-k[3] if len(k)>3 else 0)
        ready.sort(key=prio)
        comp=None
        if mm:
            st,pt,pc=mm[0]
            if not (st==0 and agleft[0]>p['hold']): comp=part_time(st,pt)
        dur=None
        if ready and ready[0][0]<=now: pick=ready[0][1]
        elif comp is not None and comp<=now and not (ready and ready[0][0]<now+p['mm_gap']): pick=("matmul",*mm.pop(0))
        else:
            times=[e[0] for e in ready]+([comp] if comp is not None and comp>now else [])
            if later and agleft[0]<=p['inj_after']: times.append(max(now,min(free[e[1]] for e in later)-p['inj'])+0.01)
            now=min(times);continue
        ops.append(pick)
        if pick[0]=="ag":
            _,st,d,h,q=pick;del due[pick];now+=p['AG'];held[st,slot_at(chips,d,h),q]=now
            if h<reach(chips,d,q,S): send(("ag",st,d,h+1,q),d);agleft[st]-=1
        elif pick[0]=="matmul":
            _,st,pt,pc=pick
            if pc<tiles: now+=p['GU']
            else:
                now+=p['DN'];scaled[st,pt,(pc-tiles)//D]=now
        elif pick[0]=="sum":
            _,st,d,h,q=pick;now+=p['SUM'];wrs.remove((st,d,h,q));due.pop(("rs",st,d,h+1,q),None);send(("rs",st,d,h,q),1-d)
        else:
            _,st,q=pick;now+=p['SUM'];wc.remove((st,q))
            for d in range(2): del due["rs",st,d,1,q]
    return ops,now

def kernel(
    chips,
    across,
    hidden_ref,
    ids_hbm,
    weights_hbm,
    gate_hbm,
    up_hbm,
    down_hbm,
    out_hbm,
    ids_ref,
    weights_ref,
    out,
    gate_sum,
    x,
    pc,
    rs,
    table,
    gate,
    up,
    down,
    mid,
    scale,
    load_sem,
    ag_s,
    ag_r,
    pf_s,
    pf_r,
    pc_s,
    pc_r,
    rs_s,
    rs_r,
    tb_s,
    tb_r,
    tp_s,
    tp_r,
    out_s,
):
    steps, _, _, rows, width = x.shape
    inner = gate.shape[1]
    experts = 2 * chips
    along = chips // across

    me = lax.axis_index("expert")
    core = lax.rem(me, 2)
    chip = lax.div(me, 2)
    if across == 2:
        far, deep = lax.rem(chip, 2), lax.div(chip, 2)
        here = (1 - far) * deep + far * (2 * along - 1 - deep)
    else:
        here = chip

    def device_at(position):
        if across == 2:
            far = lax.div(position, along)
            deep = (1 - far) * position + far * (2 * along - 1 - position)
            position = deep * 2 + far
        return {"expert": position * 2 + core}

    sign = 1 - 2 * core
    neighbours = (
        device_at(lax.rem(here + sign + chips, chips)),
        device_at(lax.rem(here - sign + chips, chips)),
    )
    partner = {"expert": chip * 2 + (1 - core)}
    slot = functools.partial(slot_at, chips)
    order = slots_in_order(chips)
    place = {s: i for i, s in enumerate(order)}
    per = chips // PARTS
    part_of = {s: i // per for i, s in enumerate(order)}
    high, wide = rows // 2, width // SIDES

    def mirror(s):
        return (chips - s) % chips

    def area(q):
        return pl.ds(q // SIDES * high, high), pl.ds(q % SIDES * wide, wide)

    def remote(src, dst, send, recv, target):
        return pltpu.make_async_remote_copy(
            src_ref=src,
            dst_ref=dst,
            send_sem=send,
            recv_sem=recv,
            device_id=target,
            device_id_type=MESH,
        )

    def ag_copy(st, d, hop, q):
        return remote(
            x.at[st, place[slot(d, hop - 1)], 0, *area(q)],
            x.at[st, place[slot(d, hop)], 0, *area(q)],
            ag_s.at[st, part_of[slot(d, hop - 1)]],
            ag_r.at[st, place[slot(d, hop)] - 1, q],
            neighbours[d],
        )

    def pf_copy(st, s, q):
        return remote(
            x.at[st, place[s], 0, *area(q)],
            x.at[st, place[mirror(s)], 1, *area(q)],
            pf_s.at[st, part_of[s]],
            pf_r.at[st, part_of[mirror(s)]],
            partner,
        )

    def pc_copy(st, s, c):
        columns = pl.ds(c * wide, wide)
        return remote(
            x.at[st, place[s], 1, :, columns],
            pc.at[st, mirror(s), :, columns],
            pc_s,
            pc_r.at[st, part_of[s], c],
            partner,
        )

    def rs_copy(st, d, hop, q):
        target = slot(d, hop - 1) if (d == 0 or hop > 1) else chips // 2
        return remote(
            x.at[st, place[slot(d, hop)], 0, *area(q)],
            rs.at[st, target, *area(q)],
            rs_s,
            rs_r.at[st, target, q],
            neighbours[1 - d],
        )

    def tb_copy(d, hop):
        return remote(
            table.at[place[slot(d, hop - 1)], 0],
            table.at[place[slot(d, hop)], 0],
            tb_s,
            tb_r.at[place[slot(d, hop)] - 1],
            neighbours[d],
        )

    def tp_copy(s):
        return remote(
            table.at[place[s], 0],
            table.at[place[mirror(s)], 1],
            tp_s,
            tp_r.at[part_of[mirror(s)]],
            partner,
        )

    barrier = pltpu.get_barrier_semaphore()
    for target in (*neighbours, partner):
        pl.semaphore_signal(barrier, inc=1, device_id=target, device_id_type=MESH)

    own = [
        pltpu.make_async_copy(hidden_ref.at[st], x.at[st, 0, 0], load_sem.at[3 + st])
        for st in range(steps)
    ]
    for copy in own:
        copy.start()
    loads = [
        pltpu.make_async_copy(src.at[0], dst, load_sem.at[i])
        for i, (src, dst) in enumerate(((gate_hbm, gate), (up_hbm, up), (down_hbm, down)))
    ]
    small = [
        pltpu.make_async_copy(src, dst, load_sem.at[3 + steps + i])
        for i, (src, dst) in enumerate(((ids_hbm, ids_ref), (weights_hbm, weights_ref)))
    ]
    for copy in small:
        copy.start()
    for copy in loads:
        copy.start()
    own[0].wait()
    pl.semaphore_wait(barrier, 3)

    lanes = table.shape[3]

    def table_open():
        for copy in small:
            copy.wait()
        label = lax.broadcasted_iota(jnp.int32, (experts, rows), 0)
        for st in range(steps):
            raw = weights_ref[st]
            normalized = raw / jnp.sum(raw, axis=0, keepdims=True)
            ids = ids_ref[st]
            dense = jnp.zeros((experts, rows), jnp.float32)
            for k in range(ids.shape[0]):
                dense = dense + jnp.where(label == ids[k : k + 1], normalized[k : k + 1], 0.0)
            table[0, 0, :, pl.ds(st * rows, rows)] = dense
        for d in range(2):
            tb_copy(d, 1).start()
        tp_copy(0).start()

    def table_event(d, hop):
        tb_copy(d, hop).wait_recv()
        if hop < reach(chips, d, 0):
            tb_copy(d, hop + 1).start()
        tp_copy(slot(d, hop)).start()

    def ag_event(st, d, hop, q):
        if st == 0 and q == 1 and hop <= reach(chips, d, 0):
            table_event(d, hop)
        ag_copy(st, d, hop, q).wait_recv()
        if hop < reach(chips, d, q):
            ag_copy(st, d, hop + 1, q).start()
        pf_copy(st, slot(d, hop), q).start()

    summed = set()

    def partner_sums(st, s, c):
        key = (st, part_of[mirror(s)], c)
        if key not in summed:
            summed.add(key)
            some = pc.at[st, pl.ds(0, per), :, pl.ds(c * wide, wide)]
            pltpu.make_async_copy(some, some, pc_r.at[key]).wait()

    def total(st, s, received, q):
        partner_sums(st, s, q % SIDES)
        value = x[st, place[s], 0, *area(q)].astype(jnp.float32)
        value = value + pc[st, s, *area(q)].astype(jnp.float32)
        for index in received:
            value = value + rs[st, index, *area(q)].astype(jnp.float32)
        return value.astype(jnp.bfloat16)

    def rs_event(st, d, hop, q):
        s = slot(d, hop)
        received = []
        if hop < reach(chips, d, q):
            rs_copy(st, d, hop + 1, q).wait_recv()
            received = [s]
        x[st, place[s], 0, *area(q)] = total(st, s, received, q)
        rs_copy(st, d, hop, q).start()

    def out_copy(st, q):
        return pltpu.make_async_copy(out.at[st, *area(q)], out_hbm.at[st, *area(q)], out_s)

    def rs_close(st, q):
        for d in range(2):
            rs_copy(st, d, 1, q).wait_recv()
        out[st, *area(q)] = total(st, 0, [0, chips // 2], q)
        out_copy(st, q).start()

    block = min(4, per)
    tall = block * 2 * rows
    ff_tile = 256 if inner % 256 == 0 else inner
    tiles = 2 * inner // ff_tile

    def over_blocks(first, body):
        if per == block:
            body(first, 0)
        else:
            def step(i, carry):
                body(first + i * block, i * tall)
                return carry

            lax.fori_loop(0, per // block, step, 0)

    def gate_up(st, part, tile):
        columns = pl.ds(tile // 2 * ff_tile, ff_tile)

        def body(first, row):
            rows_in = x[st, pl.ds(first, block)].reshape(tall, width)
            if tile % 2 == 0:
                g = jnp.dot(rows_in, gate[:, columns], preferred_element_type=jnp.float32)
                gate_sum[pl.ds(row, tall)] = g / (1.0 + jnp.exp(-g))
            else:
                u = jnp.dot(rows_in, up[:, columns], preferred_element_type=jnp.float32)
                mid[pl.ds(row, tall), columns] = (gate_sum[pl.ds(row, tall)] * u).astype(jnp.bfloat16)

        over_blocks(part * per, body)

    def fill_scale(st, part):
        if st == 0:
            some = table.at[pl.ds(0, per), 0]
            pltpu.make_async_copy(some, some, tp_r.at[part]).wait()
        spot = lax.broadcasted_iota(jnp.int32, (experts, lanes), 0)
        blocks = 2 * block
        column = lax.broadcasted_iota(jnp.int32, (tall, blocks), 1)
        group = lax.broadcasted_iota(jnp.int32, (tall, blocks), 0) // rows

        def body(first, row):
            picked = [
                jnp.sum(jnp.where(spot == me, table[first + i, c], 0.0), axis=0, keepdims=True)
                for i in range(block)
                for c in range(2)
            ]
            turned = jnp.concatenate(picked, axis=0).T[st * rows : (st + 1) * rows]
            spread = jnp.concatenate([turned] * blocks, axis=0)
            weight = jnp.sum(jnp.where(column == group, spread, 0.0), axis=1, keepdims=True)
            scale[pl.ds(row, tall), :] = jnp.broadcast_to(weight, (tall, LANES))

        over_blocks(part * per, body)

    def down_part(st, part, piece):
        c, third = piece // DOWNS, piece % DOWNS
        if piece == 0:
            fill_scale(st, part)
            onward = sum(
                hop < reach(chips, d, q)
                for d in range(2)
                for q in range(2 * SIDES)
                for hop in range(reach(chips, d, q))
                if part_of[slot(d, hop)] == part
            )
            for blocks, sem in ((onward // (2 * SIDES), ag_s), (per, pf_s)):
                some = x.at[st, pl.ds(0, blocks), 0]
                pltpu.make_async_copy(some, some, sem.at[st, part]).wait()
        start, stop = (wide // LANES * (third + i) // DOWNS * LANES for i in range(2))
        columns = pl.ds(c * wide + start, stop - start)

        def body(first, row):
            v = jnp.dot(
                mid[pl.ds(row, tall), :], down[:, columns], preferred_element_type=jnp.float32
            )
            weight = scale[pl.ds(row, tall), :]
            v = v * jnp.concatenate([weight] * ((stop - start) // LANES), axis=1)
            v = v.astype(jnp.bfloat16).reshape(block, 2, rows, stop - start)
            x[st, pl.ds(first, block), :, :, columns] = v

        over_blocks(part * per, body)
        if third == DOWNS - 1:
            for s in order[part * per : (part + 1) * per]:
                pc_copy(st, s, c).start()

    arrived = set()
    loaded = set()

    def matmul_event(st, part, piece):
        if (st, part) not in arrived:
            arrived.add((st, part))
            some = x.at[st, pl.ds(0, per), 1]
            pltpu.make_async_copy(some, some, pf_r.at[st, part]).wait()
        if not loaded:
            loaded.add(0)
            for copy in loads:
                copy.wait()
        if piece < tiles:
            gate_up(st, part, piece)
        else:
            down_part(st, part, piece - tiles)

    def own_event(st, d, q):
        if q == 0 and d == 0 and st > 0:
            own[st].wait()
        ag_copy(st, d, 1, q).start()
        if q == SIDES * 2 - 1 and d == 1:
            for c in range(2 * SIDES):
                pf_copy(st, 0, c).start()
            if st == 0:
                table_open()

    run = {
        "own": own_event,
        "ag": ag_event,
        "matmul": matmul_event,
        "sum": rs_event,
        "close": rs_close,
    }
    for name, *where in plan(chips, steps, tiles=tiles, DOWNS=DOWNS, inj=2.0, inj_after=4, mm_gap=0.2, HOP=2.5)[0]:
        run[name](*where)

    for sent, sem in (
        (x.at[:, :, 1], pc_s),
        (x.at[:, pl.ds(0, chips - 1), 0], rs_s),
        (table.at[pl.ds(0, chips - 1), 0], tb_s),
        (table.at[:, 0], tp_s),
        (out, out_s),
    ):
        pltpu.make_async_copy(sent, sent, sem).wait()


def on_device(across, hidden_states, route_ids, route_weights, gate_proj, up_proj, down_proj):
    steps, rows, width = hidden_states.shape
    experts = lax.axis_size("expert")
    inner = gate_proj.shape[2]
    chips = experts // 2
    per = chips // PARTS
    lanes = -(-steps * rows // LANES) * LANES
    dma = pltpu.SemaphoreType.DMA
    bf16 = jnp.bfloat16
    hbm = pl.BlockSpec(memory_space=pl.ANY)
    return pl.pallas_call(
        functools.partial(kernel, chips, across),
        out_shape=jax.ShapeDtypeStruct((steps, rows, width), bf16),
        in_specs=[hbm] * 6,
        out_specs=hbm,
        scratch_shapes=[
            pltpu.VMEM((steps, route_ids.shape[2], rows), jnp.int32),
            pltpu.VMEM((steps, route_ids.shape[2], rows), jnp.float32),
            pltpu.VMEM((steps, rows, width), bf16),
            pltpu.VMEM((per * 2 * rows, 256 if inner % 256 == 0 else inner), jnp.float32),
            pltpu.VMEM((steps, chips, 2, rows, width), bf16),
            pltpu.VMEM((steps, chips, rows, width), bf16),
            pltpu.VMEM((steps, chips, rows, width), bf16),
            pltpu.VMEM((chips, 2, experts, lanes), jnp.float32),
            pltpu.VMEM((width, inner), bf16),
            pltpu.VMEM((width, inner), bf16),
            pltpu.VMEM((inner, width), bf16),
            pltpu.VMEM((per * 2 * rows, inner), bf16),
            pltpu.VMEM((per * 2 * rows, LANES), jnp.float32),
            dma((5 + steps,)),
            dma((steps, PARTS)),
            dma((steps, chips - 1, 2 * SIDES)),
            dma((steps, PARTS)),
            dma((steps, PARTS)),
            dma,
            dma((steps, PARTS, SIDES)),
            dma,
            dma((steps, chips, 2 * SIDES)),
            dma,
            dma((chips - 1,)),
            dma,
            dma((PARTS,)),
            dma,
        ],
        compiler_params=pltpu.CompilerParams(
            collective_id=0, has_side_effects=True, vmem_limit_bytes=64_000_000
        ),
    )(hidden_states, route_ids.swapaxes(1, 2), route_weights.swapaxes(1, 2), gate_proj, up_proj, down_proj)


def solution(mesh):
    across = 2 if mesh.shape["groups"] == 2 else 1
    placed = (
        P(None, ("groups", "expert"), None),
        P(None, ("groups", "expert"), None),
        P(None, ("groups", "expert"), None),
        P("expert", None, None),
        P("expert", None, None),
        P("expert", None, None),
    )
    return jax.shard_map(
        functools.partial(on_device, across),
        mesh=mesh,
        in_specs=placed,
        out_specs=P(None, ("groups", "expert"), None),
        check_vma=False,
    )
```

```python
import functools
import itertools

import jax
import jax.numpy as jnp
from jax import lax
from jax.experimental import pallas as pl
from jax.experimental.pallas import tpu as pltpu
from jax.sharding import PartitionSpec as P

MESH = pl.DeviceIdType.MESH
LANES = 128
SIDES = 2
DOWNS = 5
PARTS = 2
HOP_US = 2.7
CHUNK_US = 0.9
PAIR_US = 1.5
BACK_US = 2.0
GATHER_US = 0.05
SUM_US = 0.15
GATE_UP_US = 0.5
DOWN_US = 0.4


import itertools, random
def reach(chips,d,q,S=2): return chips//2 if q//S==d else chips-1-chips//2
def slot_at(chips,d,hop): return hop if d==0 else (chips-hop)%chips
def slots_in_order(chips):
    order=[0]
    for hop in range(1,chips//2+1): order+=[s for s in dict.fromkeys((hop,chips-hop))]
    return order
DEF=dict(HOP=2.7,CHUNK=0.9,PAIR=1.5,BACK=2.0,AG=0.05,SUM=0.12,GU=0.34,DN=0.17,DOWNS=5,tiles=6,
         inj=0.2,inj_after=0,hold=0,rs_first=0,mm_gap=0.0,rs0_bias=0.0,S=2)
def plan(chips=8,steps=2,**kw):
    p=dict(DEF);p.update(kw); S=p['S']
    tiles=p['tiles'];D=p['DOWNS']
    order=slots_in_order(chips);per=chips//2
    part_of={s:i//per for i,s in enumerate(order)}
    chunks=range(2*S);ops=[];free=[0.,0.];due={};held={};now=0.
    busy=0.
    def send(key,d):
        start=max(now,free[d]);free[d]=start+p['CHUNK'];due[key]=free[d]+p['HOP']
    later=[(st,d,q) for st in range(1,steps) for q in chunks for d in range(2)]
    for q in chunks:
        for d in range(2):
            ops.append(("own",0,d,q));send(("ag",0,d,1,q),d)
    for st in range(steps):
        for q in chunks: held[st,0,q]=0.
    mm=[(st,pt,pc) for st in range(steps) for pt in range(2) for pc in range(tiles+S*D)]
    scaled={}
    wrs=[(st,d,h,q) for st in range(steps) for q in chunks for d in range(2) for h in range(reach(chips,d,q,S),0,-1)]
    wc=[(st,q) for st in range(steps) for q in chunks]
    agleft={st:sum(reach(chips,d,q,S)-1 for q in chunks for d in range(2)) for st in range(steps)}
    def part_time(st,part):
        last=0.
        for s in order[part*per:(part+1)*per]:
            for q in chunks:
                for key,ex in (((st,s,q),0.),((st,(chips-s)%chips,q),p['PAIR'])):
                    if key not in held: return None
                    last=max(last,held[key]+ex)
        return last
    def summed(st,s,q):
        a=(st,part_of[s],q%S);b=(st,part_of[(chips-s)%chips],q%S)
        if a not in scaled or b not in scaled: return None
        return max(scaled[a],scaled[b]+p['BACK'])
    while mm or wrs or wc or due:
        if agleft[0]<=p['inj_after']:
            for e in list(later):
                st,d,q=e
                if free[d]<=now+p['inj'] and not any(f[1]==d for f in later[:later.index(e)]):
                    later.remove(e);ops.append(("own",st,d,q));send(("ag",st,d,1,q),d)
        ready=[]
        for key,when in due.items():
            if key[0]=="ag": ready.append((when,key))
        for st,d,h,q in wrs:
            when=summed(st,slot_at(chips,d,h),q)
            if when is None: continue
            if h<reach(chips,d,q,S):
                if ("rs",st,d,h+1,q) not in due: continue
                when=max(when,due["rs",st,d,h+1,q])
            ready.append((when,("sum",st,d,h,q)))
        for st,q in wc:
            when=summed(st,0,q)
            if when is None or any(("rs",st,d,1,q) not in due for d in range(2)): continue
            ready.append((max([when]+[due["rs",st,d,1,q] for d in range(2)]),("close",st,q)))
        def prio(e):
            when,k=e
            cls={"ag":0,"sum":1 if not p['rs_first'] else -1,"close":5}[k[0]]
            if k[0]=="ag" and k[1]==1: cls+=0.5
            return (max(when,now),k[1],cls,when,-k[3] if len(k)>3 else 0)
        ready.sort(key=prio)
        comp=None
        if mm:
            st,pt,pc=mm[0]
            if not (st==0 and agleft[0]>p['hold']): comp=part_time(st,pt)
        dur=None
        if ready and ready[0][0]<=now: pick=ready[0][1]
        elif comp is not None and comp<=now and not (ready and ready[0][0]<now+p['mm_gap']): pick=("matmul",*mm.pop(0))
        else:
            times=[e[0] for e in ready]+([comp] if comp is not None and comp>now else [])
            if later and agleft[0]<=p['inj_after']: times.append(max(now,min(free[e[1]] for e in later)-p['inj'])+0.01)
            now=min(times);continue
        ops.append(pick)
        if pick[0]=="ag":
            _,st,d,h,q=pick;del due[pick];now+=p['AG'];held[st,slot_at(chips,d,h),q]=now
            if h<reach(chips,d,q,S): send(("ag",st,d,h+1,q),d);agleft[st]-=1
        elif pick[0]=="matmul":
            _,st,pt,pc=pick
            if pc<tiles: now+=p['GU']
            else:
                now+=p['DN'];scaled[st,pt,(pc-tiles)//D]=now
        elif pick[0]=="sum":
            _,st,d,h,q=pick;now+=p['SUM'];wrs.remove((st,d,h,q));due.pop(("rs",st,d,h+1,q),None);send(("rs",st,d,h,q),1-d)
        else:
            _,st,q=pick;now+=p['SUM'];wc.remove((st,q))
            for d in range(2): del due["rs",st,d,1,q]
    return ops,now

def kernel(
    chips,
    across,
    hidden_ref,
    ids_hbm,
    weights_hbm,
    gate_hbm,
    up_hbm,
    down_hbm,
    out,
    ids_ref,
    weights_ref,
    gate_sum,
    x,
    pc,
    rs,
    table,
    gate,
    up,
    down,
    mid,
    scale,
    load_sem,
    ag_s,
    ag_r,
    pf_s,
    pf_r,
    pc_s,
    pc_r,
    rs_s,
    rs_r,
    tb_s,
    tb_r,
    tp_s,
    tp_r,
):
    steps, _, _, rows, width = x.shape
    inner = gate.shape[1]
    experts = 2 * chips
    along = chips // across

    me = lax.axis_index("expert")
    core = lax.rem(me, 2)
    chip = lax.div(me, 2)
    if across == 2:
        far, deep = lax.rem(chip, 2), lax.div(chip, 2)
        here = (1 - far) * deep + far * (2 * along - 1 - deep)
    else:
        here = chip

    def device_at(position):
        if across == 2:
            far = lax.div(position, along)
            deep = (1 - far) * position + far * (2 * along - 1 - position)
            position = deep * 2 + far
        return {"expert": position * 2 + core}

    sign = 1 - 2 * core
    neighbours = (
        device_at(lax.rem(here + sign + chips, chips)),
        device_at(lax.rem(here - sign + chips, chips)),
    )
    partner = {"expert": chip * 2 + (1 - core)}
    slot = functools.partial(slot_at, chips)
    order = slots_in_order(chips)
    place = {s: i for i, s in enumerate(order)}
    per = chips // PARTS
    part_of = {s: i // per for i, s in enumerate(order)}
    high, wide = rows // 2, width // SIDES

    def mirror(s):
        return (chips - s) % chips

    def area(q):
        return pl.ds(q // SIDES * high, high), pl.ds(q % SIDES * wide, wide)

    def remote(src, dst, send, recv, target):
        return pltpu.make_async_remote_copy(
            src_ref=src,
            dst_ref=dst,
            send_sem=send,
            recv_sem=recv,
            device_id=target,
            device_id_type=MESH,
        )

    def ag_copy(st, d, hop, q):
        return remote(
            x.at[st, place[slot(d, hop - 1)], 0, *area(q)],
            x.at[st, place[slot(d, hop)], 0, *area(q)],
            ag_s.at[st, part_of[slot(d, hop - 1)]],
            ag_r.at[st, place[slot(d, hop)] - 1, q],
            neighbours[d],
        )

    def pf_copy(st, s, q):
        return remote(
            x.at[st, place[s], 0, *area(q)],
            x.at[st, place[mirror(s)], 1, *area(q)],
            pf_s.at[st, part_of[s]],
            pf_r.at[st, part_of[mirror(s)]],
            partner,
        )

    def pc_copy(st, s, c):
        columns = pl.ds(c * wide, wide)
        return remote(
            x.at[st, place[s], 1, :, columns],
            pc.at[st, mirror(s), :, columns],
            pc_s,
            pc_r.at[st, part_of[s], c],
            partner,
        )

    def rs_copy(st, d, hop, q):
        target = slot(d, hop - 1) if (d == 0 or hop > 1) else chips // 2
        return remote(
            x.at[st, place[slot(d, hop)], 0, *area(q)],
            rs.at[st, target, *area(q)],
            rs_s,
            rs_r.at[st, target, q],
            neighbours[1 - d],
        )

    def tb_copy(d, hop):
        return remote(
            table.at[place[slot(d, hop - 1)], 0],
            table.at[place[slot(d, hop)], 0],
            tb_s,
            tb_r.at[place[slot(d, hop)] - 1],
            neighbours[d],
        )

    def tp_copy(s):
        return remote(
            table.at[place[s], 0],
            table.at[place[mirror(s)], 1],
            tp_s,
            tp_r.at[part_of[mirror(s)]],
            partner,
        )

    barrier = pltpu.get_barrier_semaphore()
    for target in (*neighbours, partner):
        pl.semaphore_signal(barrier, inc=1, device_id=target, device_id_type=MESH)

    own = [
        pltpu.make_async_copy(hidden_ref.at[st], x.at[st, 0, 0], load_sem.at[3 + st])
        for st in range(steps)
    ]
    for copy in own:
        copy.start()
    loads = [
        pltpu.make_async_copy(src.at[0], dst, load_sem.at[i])
        for i, (src, dst) in enumerate(((gate_hbm, gate), (up_hbm, up), (down_hbm, down)))
    ]
    small = [
        pltpu.make_async_copy(src, dst, load_sem.at[3 + steps + i])
        for i, (src, dst) in enumerate(((ids_hbm, ids_ref), (weights_hbm, weights_ref)))
    ]
    for copy in small:
        copy.start()
    for copy in loads:
        copy.start()
    own[0].wait()
    pl.semaphore_wait(barrier, 3)

    listed, lanes = table.shape[2:]

    def table_open():
        for copy in small:
            copy.wait()
        label = lax.broadcasted_iota(jnp.int32, (experts, rows), 0)
        for st in range(steps):
            raw = weights_ref[st]
            normalized = raw / jnp.sum(raw, axis=0, keepdims=True)
            ids = ids_ref[st]
            dense = jnp.zeros((experts, rows), jnp.float32)
            for k in range(ids.shape[0]):
                dense = dense + jnp.where(label == ids[k : k + 1], normalized[k : k + 1], 0.0)
            for g in range(experts // listed):
                lane = (g * steps + st) * rows
                table[0, 0, :, pl.ds(lane, rows)] = dense[g * listed : (g + 1) * listed]
        for d in range(2):
            tb_copy(d, 1).start()
        tp_copy(0).start()

    def table_event(d, hop):
        tb_copy(d, hop).wait_recv()
        if hop < reach(chips, d, 0):
            tb_copy(d, hop + 1).start()
        tp_copy(slot(d, hop)).start()

    def ag_event(st, d, hop, q):
        if st == 0 and q == 1 and hop <= reach(chips, d, 0):
            table_event(d, hop)
        ag_copy(st, d, hop, q).wait_recv()
        if hop < reach(chips, d, q):
            ag_copy(st, d, hop + 1, q).start()
        pf_copy(st, slot(d, hop), q).start()

    summed = set()

    def partner_sums(st, s, c):
        key = (st, part_of[mirror(s)], c)
        if key not in summed:
            summed.add(key)
            some = pc.at[st, pl.ds(0, per), :, pl.ds(c * wide, wide)]
            pltpu.make_async_copy(some, some, pc_r.at[key]).wait()

    def total(st, s, received, q):
        partner_sums(st, s, q % SIDES)
        value = x[st, place[s], 0, *area(q)].astype(jnp.float32)
        value = value + pc[st, s, *area(q)].astype(jnp.float32)
        for index in received:
            value = value + rs[st, index, *area(q)].astype(jnp.float32)
        return value.astype(jnp.bfloat16)

    def rs_event(st, d, hop, q):
        s = slot(d, hop)
        received = []
        if hop < reach(chips, d, q):
            rs_copy(st, d, hop + 1, q).wait_recv()
            received = [s]
        x[st, place[s], 0, *area(q)] = total(st, s, received, q)
        rs_copy(st, d, hop, q).start()

    def rs_close(st, q):
        for d in range(2):
            rs_copy(st, d, 1, q).wait_recv()
        out[st, *area(q)] = total(st, 0, [0, chips // 2], q)

    block = min(4, per)
    tall = block * 2 * rows
    ff_tile = 256 if inner % 256 == 0 else inner
    tiles = 2 * inner // ff_tile

    def over_blocks(first, body):
        if per == block:
            body(first, 0)
        else:
            def step(i, carry):
                body(first + i * block, i * tall)
                return carry

            lax.fori_loop(0, per // block, step, 0)

    def gate_up(st, part, tile):
        columns = pl.ds(tile // 2 * ff_tile, ff_tile)

        def body(first, row):
            rows_in = x[st, pl.ds(first, block)].reshape(tall, width)
            if tile % 2 == 0:
                g = jnp.dot(rows_in, gate[:, columns], preferred_element_type=jnp.float32)
                gate_sum[pl.ds(row, tall)] = g / (1.0 + jnp.exp(-g))
            else:
                u = jnp.dot(rows_in, up[:, columns], preferred_element_type=jnp.float32)
                mid[pl.ds(row, tall), columns] = (gate_sum[pl.ds(row, tall)] * u).astype(jnp.bfloat16)

        over_blocks(part * per, body)

    def fill_scale(st, part):
        if st == 0:
            some = table.at[pl.ds(0, per), 0]
            pltpu.make_async_copy(some, some, tp_r.at[part]).wait()
        spot = lax.broadcasted_iota(jnp.int32, (listed, lanes), 0)
        mine, beside = lax.rem(me, listed), lax.div(me, listed)
        blocks = 2 * block
        column = lax.broadcasted_iota(jnp.int32, (tall, blocks), 1)
        group = lax.broadcasted_iota(jnp.int32, (tall, blocks), 0) // rows

        def body(first, row):
            picked = [
                jnp.sum(jnp.where(spot == mine, table[first + i, c], 0.0), axis=0, keepdims=True)
                for i in range(block)
                for c in range(2)
            ]
            turned = jnp.concatenate(picked, axis=0).T
            own_rows = sum(
                jnp.where(beside == g, turned[lane : lane + rows], 0.0)
                for g in range(experts // listed)
                for lane in ((g * steps + st) * rows,)
            )
            spread = jnp.concatenate([own_rows] * blocks, axis=0)
            weight = jnp.sum(jnp.where(column == group, spread, 0.0), axis=1, keepdims=True)
            scale[pl.ds(row, tall), :] = jnp.broadcast_to(weight, (tall, LANES))

        over_blocks(part * per, body)

    def down_part(st, part, piece):
        c, third = piece // DOWNS, piece % DOWNS
        if piece == 0:
            fill_scale(st, part)
            onward = sum(
                hop < reach(chips, d, q)
                for d in range(2)
                for q in range(2 * SIDES)
                for hop in range(reach(chips, d, q))
                if part_of[slot(d, hop)] == part
            )
            for blocks, sem in ((onward // (2 * SIDES), ag_s), (per, pf_s)):
                some = x.at[st, pl.ds(0, blocks), 0]
                pltpu.make_async_copy(some, some, sem.at[st, part]).wait()
        start, stop = (wide // LANES * (third + i) // DOWNS * LANES for i in range(2))
        columns = pl.ds(c * wide + start, stop - start)

        def body(first, row):
            v = jnp.dot(
                mid[pl.ds(row, tall), :], down[:, columns], preferred_element_type=jnp.float32
            )
            weight = scale[pl.ds(row, tall), :]
            v = v * jnp.concatenate([weight] * ((stop - start) // LANES), axis=1)
            v = v.astype(jnp.bfloat16).reshape(block, 2, rows, stop - start)
            x[st, pl.ds(first, block), :, :, columns] = v

        over_blocks(part * per, body)
        if third == DOWNS - 1:
            for s in order[part * per : (part + 1) * per]:
                pc_copy(st, s, c).start()

    arrived = set()
    loaded = set()

    def matmul_event(st, part, piece):
        if (st, part) not in arrived:
            arrived.add((st, part))
            some = x.at[st, pl.ds(0, per), 1]
            pltpu.make_async_copy(some, some, pf_r.at[st, part]).wait()
        if not loaded:
            loaded.add(0)
            for copy in loads:
                copy.wait()
        if piece < tiles:
            gate_up(st, part, piece)
        else:
            down_part(st, part, piece - tiles)

    def own_event(st, d, q):
        if q == 0 and d == 0 and st > 0:
            own[st].wait()
        ag_copy(st, d, 1, q).start()
        if q == SIDES * 2 - 1 and d == 1:
            for c in range(2 * SIDES):
                pf_copy(st, 0, c).start()
            if st == 0:
                table_open()

    run = {
        "own": own_event,
        "ag": ag_event,
        "matmul": matmul_event,
        "sum": rs_event,
        "close": rs_close,
    }
    for name, *where in plan(chips, steps, tiles=tiles, DOWNS=DOWNS, inj=2.0, inj_after=4, mm_gap=0.2, HOP=2.0)[0]:
        run[name](*where)

    for sent, sem in (
        (x.at[:, :, 1], pc_s),
        (x.at[:, pl.ds(0, chips - 1), 0], rs_s),
        (table.at[pl.ds(0, chips - 1), 0], tb_s),
        (table.at[:, 0], tp_s),
    ):
        pltpu.make_async_copy(sent, sent, sem).wait()


def on_device(across, hidden_states, route_ids, route_weights, gate_proj, up_proj, down_proj):
    steps, rows, width = hidden_states.shape
    experts = lax.axis_size("expert")
    inner = gate_proj.shape[2]
    chips = experts // 2
    per = chips // PARTS
    beside = max(1, LANES // (steps * rows))
    beside = beside if experts % (8 * beside) == 0 else 1
    lanes = -(-steps * rows * beside // LANES) * LANES
    dma = pltpu.SemaphoreType.DMA
    bf16 = jnp.bfloat16
    hbm = pl.BlockSpec(memory_space=pl.ANY)
    return pl.pallas_call(
        functools.partial(kernel, chips, across),
        out_shape=pltpu.VMEM((steps, rows, width), bf16),
        in_specs=[hbm] * 6,
        out_specs=pl.BlockSpec(memory_space=pltpu.VMEM),
        scratch_shapes=[
            pltpu.VMEM((steps, route_ids.shape[2], rows), jnp.int32),
            pltpu.VMEM((steps, route_ids.shape[2], rows), jnp.float32),
            pltpu.VMEM((per * 2 * rows, 256 if inner % 256 == 0 else inner), jnp.float32),
            pltpu.VMEM((steps, chips, 2, rows, width), bf16),
            pltpu.VMEM((steps, chips, rows, width), bf16),
            pltpu.VMEM((steps, chips, rows, width), bf16),
            pltpu.VMEM((chips, 2, experts // beside, lanes), jnp.float32),
            pltpu.VMEM((width, inner), bf16),
            pltpu.VMEM((width, inner), bf16),
            pltpu.VMEM((inner, width), bf16),
            pltpu.VMEM((per * 2 * rows, inner), bf16),
            pltpu.VMEM((per * 2 * rows, LANES), jnp.float32),
            dma((5 + steps,)),
            dma((steps, PARTS)),
            dma((steps, chips - 1, 2 * SIDES)),
            dma((steps, PARTS)),
            dma((steps, PARTS)),
            dma,
            dma((steps, PARTS, SIDES)),
            dma,
            dma((steps, chips, 2 * SIDES)),
            dma,
            dma((chips - 1,)),
            dma,
            dma((PARTS,)),
        ],
        compiler_params=pltpu.CompilerParams(
            collective_id=0, has_side_effects=True, vmem_limit_bytes=64_000_000
        ),
    )(hidden_states, route_ids.swapaxes(1, 2), route_weights.swapaxes(1, 2), gate_proj, up_proj, down_proj)


def solution(mesh):
    across = 2 if mesh.shape["groups"] == 2 else 1
    placed = (
        P(None, ("groups", "expert"), None),
        P(None, ("groups", "expert"), None),
        P(None, ("groups", "expert"), None),
        P("expert", None, None),
        P("expert", None, None),
        P("expert", None, None),
    )
    return jax.shard_map(
        functools.partial(on_device, across),
        mesh=mesh,
        in_specs=placed,
        out_specs=P(None, ("groups", "expert"), None),
        check_vma=False,
    )
```

```python
import functools

import jax
import jax.numpy as jnp
from jax import lax
from jax.experimental import pallas as pl
from jax.experimental.pallas import tpu as pltpu
from jax.sharding import PartitionSpec as P

MESH = pl.DeviceIdType.MESH
LANES = 128
SIDES = 2
DOWNS = 5
PARTS = 2
HOP_US = 1.6
CHUNK_US = 0.9
PAIR_US = 1.5
BACK_US = 2.0
GATHER_US = 0.05
SUM_US = 0.12
GATE_UP_US = 0.34
DOWN_US = 0.17
GAP_US = 0.2
QUEUE_US = 2.0
ONWARD = 4
HOLD = 99


def reach(chips, d, q):
    return chips // 2 if q // SIDES == d else chips - 1 - chips // 2


def slot_at(chips, d, hop):
    return hop if d == 0 else (chips - hop) % chips


def slots_in_order(chips):
    order = [0]
    for hop in range(1, chips // 2 + 1):
        order += dict.fromkeys((hop, chips - hop))
    return order


def plan(chips, steps, tiles):
    order = slots_in_order(chips)
    per = chips // PARTS
    part_of = {s: i // per for i, s in enumerate(order)}
    chunks = range(2 * SIDES)
    ops, free, due, held, scaled, now = [], [0.0, 0.0], {}, {}, {}, 0.0
    hops = [(d, q, reach(chips, d, q)) for q in chunks for d in range(2)]
    own = [(st, d, q) for st in range(1, steps) for q in chunks for d in range(2)]
    matmuls = [
        (st, part, piece)
        for st in range(steps)
        for part in range(PARTS)
        for piece in range(tiles + SIDES * DOWNS)
    ]
    sums = [(st, d, hop, q) for st in range(steps) for d, q, far in hops for hop in range(far, 0, -1)]
    closes = [(st, q) for st in range(steps) for q in chunks]
    onward = sum(far - 1 for _, _, far in hops)

    def mirror(s):
        return (chips - s) % chips

    def send(key, d):
        free[d] = max(now, free[d]) + CHUNK_US
        due[key] = free[d] + HOP_US

    def arrived(st, part):
        times = []
        for s in order[part * per : (part + 1) * per]:
            for q in chunks:
                if (st, s, q) not in held or (st, mirror(s), q) not in held:
                    return None
                times += [held[st, s, q], held[st, mirror(s), q] + PAIR_US]
        return max(times)

    def returned(st, s, q):
        mine, theirs = (st, part_of[s], q % SIDES), (st, part_of[mirror(s)], q % SIDES)
        if mine not in scaled or theirs not in scaled:
            return None
        return max(scaled[mine], scaled[theirs] + BACK_US)

    def rank(event):
        when, key = event
        later = {"ag": key[1] * 0.5, "sum": 1, "close": 5}[key[0]]
        return max(when, now), key[1], later, when, -key[3] if len(key) > 3 else 0

    for d, q, _ in hops:
        ops.append(("own", 0, d, q))
        send(("ag", 0, d, 1, q), d)
    for st in range(steps):
        held.update({(st, 0, q): 0.0 for q in chunks})

    while matmuls or sums or closes or due:
        if onward <= ONWARD:
            for st, d, q in list(own):
                first = next(entry for entry in own if entry[1] == d) == (st, d, q)
                if first and free[d] <= now + QUEUE_US:
                    own.remove((st, d, q))
                    ops.append(("own", st, d, q))
                    send(("ag", st, d, 1, q), d)
        ready = [(when, key) for key, when in due.items() if key[0] == "ag"]
        for st, d, hop, q in sums:
            when = returned(st, slot_at(chips, d, hop), q)
            before = ("rs", st, d, hop + 1, q)
            if when is None or (hop < reach(chips, d, q) and before not in due):
                continue
            ready.append((max(when, due.get(before, 0.0)), ("sum", st, d, hop, q)))
        for st, q in closes:
            when = returned(st, 0, q)
            last = [due.get(("rs", st, d, 1, q)) for d in range(2)]
            if when is not None and None not in last:
                ready.append((max(when, *last), ("close", st, q)))
        ready.sort(key=rank)
        start = None
        if matmuls and (matmuls[0][0] > 0 or onward <= HOLD):
            start = arrived(*matmuls[0][:2])
        if ready and ready[0][0] <= now:
            pick = ready[0][1]
        elif start is not None and start <= now and not (ready and ready[0][0] < now + GAP_US):
            pick = ("matmul", *matmuls.pop(0))
        else:
            times = [when for when, _ in ready]
            if start is not None and start > now:
                times.append(start)
            if own and onward <= ONWARD:
                times.append(max(now, min(free[d] for _, d, _ in own) - QUEUE_US) + 0.01)
            now = min(times)
            continue
        ops.append(pick)
        kind, st, *rest = pick
        if kind == "ag":
            d, hop, q = rest
            del due[pick]
            now += GATHER_US
            held[st, slot_at(chips, d, hop), q] = now
            if hop < reach(chips, d, q):
                send(("ag", st, d, hop + 1, q), d)
                onward -= st == 0
        elif kind == "matmul":
            part, piece = rest
            if piece < tiles:
                now += GATE_UP_US
            else:
                now += DOWN_US
                scaled[st, part, (piece - tiles) // DOWNS] = now
        elif kind == "sum":
            d, hop, q = rest
            now += SUM_US
            sums.remove((st, d, hop, q))
            due.pop(("rs", st, d, hop + 1, q), None)
            send(("rs", st, d, hop, q), 1 - d)
        else:
            now += SUM_US
            closes.remove((st, *rest))
            for d in range(2):
                del due["rs", st, d, 1, *rest]
    return ops


def kernel(
    chips,
    across,
    hidden_ref,
    ids_hbm,
    weights_hbm,
    gate_hbm,
    up_hbm,
    down_hbm,
    out,
    ids_ref,
    weights_ref,
    gate_sum,
    x,
    pc,
    rs,
    table,
    gate,
    up,
    down,
    mid,
    scale,
    load_sem,
    ag_s,
    ag_r,
    pf_s,
    pf_r,
    pc_s,
    pc_r,
    rs_s,
    rs_r,
    tb_s,
    tb_r,
    tp_s,
    tp_r,
):
    steps, _, _, rows, width = x.shape
    inner = gate.shape[1]
    experts = 2 * chips
    along = chips // across

    me = lax.axis_index("expert")
    core = lax.rem(me, 2)
    chip = lax.div(me, 2)
    if across == 2:
        far, deep = lax.rem(chip, 2), lax.div(chip, 2)
        here = (1 - far) * deep + far * (2 * along - 1 - deep)
    else:
        here = chip

    def device_at(position):
        if across == 2:
            far = lax.div(position, along)
            deep = (1 - far) * position + far * (2 * along - 1 - position)
            position = deep * 2 + far
        return {"expert": position * 2 + core}

    sign = 1 - 2 * core
    neighbours = (
        device_at(lax.rem(here + sign + chips, chips)),
        device_at(lax.rem(here - sign + chips, chips)),
    )
    partner = {"expert": chip * 2 + (1 - core)}
    slot = functools.partial(slot_at, chips)
    order = slots_in_order(chips)
    place = {s: i for i, s in enumerate(order)}
    per = chips // PARTS
    part_of = {s: i // per for i, s in enumerate(order)}
    high, wide = rows // 2, width // SIDES

    def mirror(s):
        return (chips - s) % chips

    def area(q):
        return pl.ds(q // SIDES * high, high), pl.ds(q % SIDES * wide, wide)

    def remote(src, dst, send, recv, target):
        return pltpu.make_async_remote_copy(
            src_ref=src,
            dst_ref=dst,
            send_sem=send,
            recv_sem=recv,
            device_id=target,
            device_id_type=MESH,
        )

    def ag_copy(st, d, hop, q):
        return remote(
            x.at[st, place[slot(d, hop - 1)], 0, *area(q)],
            x.at[st, place[slot(d, hop)], 0, *area(q)],
            ag_s.at[st, part_of[slot(d, hop - 1)]],
            ag_r.at[st, place[slot(d, hop)] - 1, q],
            neighbours[d],
        )

    def pf_copy(st, s, q):
        return remote(
            x.at[st, place[s], 0, *area(q)],
            x.at[st, place[mirror(s)], 1, *area(q)],
            pf_s.at[st, part_of[s]],
            pf_r.at[st, part_of[mirror(s)]],
            partner,
        )

    def pc_copy(st, s, c):
        columns = pl.ds(c * wide, wide)
        return remote(
            x.at[st, place[s], 1, :, columns],
            pc.at[st, mirror(s), :, columns],
            pc_s,
            pc_r.at[st, part_of[s], c],
            partner,
        )

    def rs_copy(st, d, hop, q):
        target = slot(d, hop - 1) if (d == 0 or hop > 1) else chips // 2
        return remote(
            x.at[st, place[slot(d, hop)], 0, *area(q)],
            rs.at[st, target, *area(q)],
            rs_s,
            rs_r.at[st, target, q],
            neighbours[1 - d],
        )

    def tb_copy(d, hop):
        return remote(
            table.at[place[slot(d, hop - 1)], 0],
            table.at[place[slot(d, hop)], 0],
            tb_s,
            tb_r.at[place[slot(d, hop)] - 1],
            neighbours[d],
        )

    def tp_copy(s):
        return remote(
            table.at[place[s], 0],
            table.at[place[mirror(s)], 1],
            tp_s,
            tp_r.at[part_of[mirror(s)]],
            partner,
        )

    barrier = pltpu.get_barrier_semaphore()
    for target in (*neighbours, partner):
        pl.semaphore_signal(barrier, inc=1, device_id=target, device_id_type=MESH)

    own = [
        pltpu.make_async_copy(hidden_ref.at[st], x.at[st, 0, 0], load_sem.at[3 + st])
        for st in range(steps)
    ]
    for copy in own:
        copy.start()
    loads = [
        pltpu.make_async_copy(src.at[0], dst, load_sem.at[i])
        for i, (src, dst) in enumerate(((gate_hbm, gate), (up_hbm, up), (down_hbm, down)))
    ]
    small = [
        pltpu.make_async_copy(src, dst, load_sem.at[3 + steps + i])
        for i, (src, dst) in enumerate(((ids_hbm, ids_ref), (weights_hbm, weights_ref)))
    ]
    for copy in small:
        copy.start()
    for copy in loads:
        copy.start()
    pl.semaphore_wait(barrier, 3)

    listed, lanes = table.shape[2:]

    def table_open():
        for copy in small:
            copy.wait()
        label = lax.broadcasted_iota(jnp.int32, (experts, rows), 0)
        for st in range(steps):
            raw = weights_ref[st]
            normalized = raw / jnp.sum(raw, axis=0, keepdims=True)
            ids = ids_ref[st]
            dense = jnp.zeros((experts, rows), jnp.float32)
            for k in range(ids.shape[0]):
                dense = dense + jnp.where(label == ids[k : k + 1], normalized[k : k + 1], 0.0)
            for g in range(experts // listed):
                lane = (g * steps + st) * rows
                table[0, 0, :, pl.ds(lane, rows)] = dense[g * listed : (g + 1) * listed]
        for d in range(2):
            tb_copy(d, 1).start()
        tp_copy(0).start()

    def table_event(d, hop):
        tb_copy(d, hop).wait_recv()
        if hop < reach(chips, d, 0):
            tb_copy(d, hop + 1).start()
        tp_copy(slot(d, hop)).start()

    def ag_event(st, d, hop, q):
        if st == 0 and q == 1 and hop <= reach(chips, d, 0):
            table_event(d, hop)
        ag_copy(st, d, hop, q).wait_recv()
        if hop < reach(chips, d, q):
            ag_copy(st, d, hop + 1, q).start()
        pf_copy(st, slot(d, hop), q).start()

    summed = set()

    def partner_sums(st, s, c):
        key = (st, part_of[mirror(s)], c)
        if key not in summed:
            summed.add(key)
            some = pc.at[st, pl.ds(0, per), :, pl.ds(c * wide, wide)]
            pltpu.make_async_copy(some, some, pc_r.at[key]).wait()

    def total(st, s, received, q):
        partner_sums(st, s, q % SIDES)
        value = x[st, place[s], 0, *area(q)].astype(jnp.float32)
        value = value + pc[st, s, *area(q)].astype(jnp.float32)
        for index in received:
            value = value + rs[st, index, *area(q)].astype(jnp.float32)
        return value.astype(jnp.bfloat16)

    def rs_event(st, d, hop, q):
        s = slot(d, hop)
        received = []
        if hop < reach(chips, d, q):
            rs_copy(st, d, hop + 1, q).wait_recv()
            received = [s]
        x[st, place[s], 0, *area(q)] = total(st, s, received, q)
        rs_copy(st, d, hop, q).start()

    def rs_close(st, q):
        for d in range(2):
            rs_copy(st, d, 1, q).wait_recv()
        out[st, *area(q)] = total(st, 0, [0, chips // 2], q)

    block = min(4, per)
    tall = block * 2 * rows
    ff_tile = 256 if inner % 256 == 0 else inner
    tiles = 2 * inner // ff_tile

    def over_blocks(first, body):
        if per == block:
            body(first, 0)
        else:
            def step(i, carry):
                body(first + i * block, i * tall)
                return carry

            lax.fori_loop(0, per // block, step, 0)

    def gate_up(st, part, tile):
        columns = pl.ds(tile // 2 * ff_tile, ff_tile)

        def body(first, row):
            rows_in = x[st, pl.ds(first, block)].reshape(tall, width)
            if tile % 2 == 0:
                g = jnp.dot(rows_in, gate[:, columns], preferred_element_type=jnp.float32)
                gate_sum[pl.ds(row, tall)] = g / (1.0 + jnp.exp(-g))
            else:
                u = jnp.dot(rows_in, up[:, columns], preferred_element_type=jnp.float32)
                mid[pl.ds(row, tall), columns] = (gate_sum[pl.ds(row, tall)] * u).astype(jnp.bfloat16)

        over_blocks(part * per, body)

    def fill_scale(st, part):
        if st == 0:
            some = table.at[pl.ds(0, per), 0]
            pltpu.make_async_copy(some, some, tp_r.at[part]).wait()
        spot = lax.broadcasted_iota(jnp.int32, (listed, lanes), 0)
        mine, beside = lax.rem(me, listed), lax.div(me, listed)
        blocks = 2 * block
        column = lax.broadcasted_iota(jnp.int32, (tall, blocks), 1)
        group = lax.broadcasted_iota(jnp.int32, (tall, blocks), 0) // rows

        def body(first, row):
            picked = [
                jnp.sum(jnp.where(spot == mine, table[first + i, c], 0.0), axis=0, keepdims=True)
                for i in range(block)
                for c in range(2)
            ]
            turned = jnp.concatenate(picked, axis=0).T
            own_rows = sum(
                jnp.where(beside == g, turned[lane : lane + rows], 0.0)
                for g in range(experts // listed)
                for lane in ((g * steps + st) * rows,)
            )
            spread = jnp.concatenate([own_rows] * blocks, axis=0)
            weight = jnp.sum(jnp.where(column == group, spread, 0.0), axis=1, keepdims=True)
            scale[pl.ds(row, tall), :] = jnp.broadcast_to(weight, (tall, LANES))

        over_blocks(part * per, body)

    def down_part(st, part, piece):
        c, third = piece // DOWNS, piece % DOWNS
        if piece == 0:
            fill_scale(st, part)
            onward = sum(
                hop < reach(chips, d, q)
                for d in range(2)
                for q in range(2 * SIDES)
                for hop in range(reach(chips, d, q))
                if part_of[slot(d, hop)] == part
            )
            for blocks, sem in ((onward // (2 * SIDES), ag_s), (per, pf_s)):
                some = x.at[st, pl.ds(0, blocks), 0]
                pltpu.make_async_copy(some, some, sem.at[st, part]).wait()
        start, stop = (wide // LANES * (third + i) // DOWNS * LANES for i in range(2))
        columns = pl.ds(c * wide + start, stop - start)

        def body(first, row):
            v = jnp.dot(
                mid[pl.ds(row, tall), :], down[:, columns], preferred_element_type=jnp.float32
            )
            weight = scale[pl.ds(row, tall), :]
            v = v * jnp.concatenate([weight] * ((stop - start) // LANES), axis=1)
            v = v.astype(jnp.bfloat16).reshape(block, 2, rows, stop - start)
            x[st, pl.ds(first, block), :, :, columns] = v

        over_blocks(part * per, body)
        if third == DOWNS - 1:
            for s in order[part * per : (part + 1) * per]:
                pc_copy(st, s, c).start()

    arrived = set()
    loaded = set()

    def matmul_event(st, part, piece):
        if (st, part) not in arrived:
            arrived.add((st, part))
            some = x.at[st, pl.ds(0, per), 1]
            pltpu.make_async_copy(some, some, pf_r.at[st, part]).wait()
        if not loaded:
            loaded.add(0)
            for copy in loads:
                copy.wait()
        if piece < tiles:
            gate_up(st, part, piece)
        else:
            down_part(st, part, piece - tiles)

    begun = set()

    def own_event(st, d, q):
        if st not in begun:
            begun.add(st)
            own[st].wait()
        ag_copy(st, d, 1, q).start()
        if q == SIDES * 2 - 1 and d == 1:
            for c in range(2 * SIDES):
                pf_copy(st, 0, c).start()
            if st == 0:
                table_open()

    run = {
        "own": own_event,
        "ag": ag_event,
        "matmul": matmul_event,
        "sum": rs_event,
        "close": rs_close,
    }
    for name, *where in plan(chips, steps, tiles):
        run[name](*where)

    for sent, sem in (
        (x.at[:, :, 1], pc_s),
        (x.at[:, pl.ds(0, chips - 1), 0], rs_s),
        (table.at[pl.ds(0, chips - 1), 0], tb_s),
        (table.at[:, 0], tp_s),
    ):
        pltpu.make_async_copy(sent, sent, sem).wait()


def on_device(across, hidden_states, route_ids, route_weights, gate_proj, up_proj, down_proj):
    steps, rows, width = hidden_states.shape
    experts = lax.axis_size("expert")
    inner = gate_proj.shape[2]
    chips = experts // 2
    per = chips // PARTS
    beside = max(1, LANES // (steps * rows))
    beside = beside if experts % (8 * beside) == 0 else 1
    lanes = -(-steps * rows * beside // LANES) * LANES
    dma = pltpu.SemaphoreType.DMA
    bf16 = jnp.bfloat16
    hbm = pl.BlockSpec(memory_space=pl.ANY)
    return pl.pallas_call(
        functools.partial(kernel, chips, across),
        out_shape=pltpu.VMEM((steps, rows, width), bf16),
        in_specs=[hbm] * 6,
        out_specs=pl.BlockSpec(memory_space=pltpu.VMEM),
        scratch_shapes=[
            pltpu.VMEM((steps, route_ids.shape[2], rows), jnp.int32),
            pltpu.VMEM((steps, route_ids.shape[2], rows), jnp.float32),
            pltpu.VMEM((per * 2 * rows, 256 if inner % 256 == 0 else inner), jnp.float32),
            pltpu.VMEM((steps, chips, 2, rows, width), bf16),
            pltpu.VMEM((steps, chips, rows, width), bf16),
            pltpu.VMEM((steps, chips, rows, width), bf16),
            pltpu.VMEM((chips, 2, experts // beside, lanes), jnp.float32),
            pltpu.VMEM((width, inner), bf16),
            pltpu.VMEM((width, inner), bf16),
            pltpu.VMEM((inner, width), bf16),
            pltpu.VMEM((per * 2 * rows, inner), bf16),
            pltpu.VMEM((per * 2 * rows, LANES), jnp.float32),
            dma((5 + steps,)),
            dma((steps, PARTS)),
            dma((steps, chips - 1, 2 * SIDES)),
            dma((steps, PARTS)),
            dma((steps, PARTS)),
            dma,
            dma((steps, PARTS, SIDES)),
            dma,
            dma((steps, chips, 2 * SIDES)),
            dma,
            dma((chips - 1,)),
            dma,
            dma((PARTS,)),
        ],
        compiler_params=pltpu.CompilerParams(
            collective_id=0, has_side_effects=True, vmem_limit_bytes=64_000_000
        ),
    )(hidden_states, route_ids.swapaxes(1, 2), route_weights.swapaxes(1, 2), gate_proj, up_proj, down_proj)


def solution(mesh):
    across = 2 if mesh.shape["groups"] == 2 else 1
    placed = (
        P(None, ("groups", "expert"), None),
        P(None, ("groups", "expert"), None),
        P(None, ("groups", "expert"), None),
        P("expert", None, None),
        P("expert", None, None),
        P("expert", None, None),
    )
    return jax.shard_map(
        functools.partial(on_device, across),
        mesh=mesh,
        in_specs=placed,
        out_specs=P(None, ("groups", "expert"), None),
        check_vma=False,
    )
```

```python
import functools

import jax
import jax.numpy as jnp
from jax import lax
from jax.experimental import pallas as pl
from jax.experimental.pallas import tpu as pltpu
from jax.sharding import PartitionSpec as P

MESH = pl.DeviceIdType.MESH
LANES = 128
SIDES = 2
DOWNS = 5
PARTS = 2
HOP_US = 1.6
CHUNK_US = 0.9
PAIR_US = 1.5
BACK_US = 2.0
GATHER_US = 0.05
SUM_US = 0.12
GATE_UP_US = 0.34
DOWN_US = 0.17
GAP_US = 0.2
QUEUE_US = 2.0
ONWARD = 2
HOLD = 99


def reach(chips, d, q):
    return chips // 2 if q // SIDES == d else chips - 1 - chips // 2


def slot_at(chips, d, hop):
    return hop if d == 0 else (chips - hop) % chips


def slots_in_order(chips):
    order = [0]
    for hop in range(1, chips // 2 + 1):
        order += dict.fromkeys((hop, chips - hop))
    return order


def plan(chips, steps, tiles):
    order = slots_in_order(chips)
    per = chips // PARTS
    part_of = {s: i // per for i, s in enumerate(order)}
    chunks = range(2 * SIDES)
    ops, free, due, held, scaled, now = [], [0.0, 0.0], {}, {}, {}, 0.0
    hops = [(d, q, reach(chips, d, q)) for q in chunks for d in range(2)]
    own = [(st, d, q) for st in range(1, steps) for q in chunks for d in range(2)]
    matmuls = [
        (st, part, piece)
        for st in range(steps)
        for part in range(PARTS)
        for piece in range(tiles + SIDES * DOWNS)
    ]
    sums = [(st, d, hop, q) for st in range(steps) for d, q, far in hops for hop in range(far, 0, -1)]
    closes = [(st, q) for st in range(steps) for q in chunks]
    onward = sum(far - 1 for _, _, far in hops)

    def mirror(s):
        return (chips - s) % chips

    def send(key, d):
        free[d] = max(now, free[d]) + CHUNK_US
        due[key] = free[d] + HOP_US

    def arrived(st, part):
        times = []
        for s in order[part * per : (part + 1) * per]:
            for q in chunks:
                if (st, s, q) not in held or (st, mirror(s), q) not in held:
                    return None
                times += [held[st, s, q], held[st, mirror(s), q] + PAIR_US]
        return max(times)

    def returned(st, s, q):
        mine, theirs = (st, part_of[s], q % SIDES), (st, part_of[mirror(s)], q % SIDES)
        if mine not in scaled or theirs not in scaled:
            return None
        return max(scaled[mine], scaled[theirs] + BACK_US)

    def rank(event):
        when, key = event
        later = {"ag": key[1] * 0.5, "sum": 1, "close": 5}[key[0]]
        return max(when, now), key[1], later, when, -key[3] if len(key) > 3 else 0

    for d, q, _ in hops:
        ops.append(("own", 0, d, q))
        send(("ag", 0, d, 1, q), d)
    for st in range(steps):
        held.update({(st, 0, q): 0.0 for q in chunks})

    while matmuls or sums or closes or due:
        if onward <= ONWARD:
            for st, d, q in list(own):
                first = next(entry for entry in own if entry[1] == d) == (st, d, q)
                if first and free[d] <= now + QUEUE_US:
                    own.remove((st, d, q))
                    ops.append(("own", st, d, q))
                    send(("ag", st, d, 1, q), d)
        ready = [(when, key) for key, when in due.items() if key[0] == "ag"]
        for st, d, hop, q in sums:
            when = returned(st, slot_at(chips, d, hop), q)
            before = ("rs", st, d, hop + 1, q)
            if when is None or (hop < reach(chips, d, q) and before not in due):
                continue
            ready.append((max(when, due.get(before, 0.0)), ("sum", st, d, hop, q)))
        for st, q in closes:
            when = returned(st, 0, q)
            last = [due.get(("rs", st, d, 1, q)) for d in range(2)]
            if when is not None and None not in last:
                ready.append((max(when, *last), ("close", st, q)))
        ready.sort(key=rank)
        start = None
        if matmuls and (matmuls[0][0] > 0 or onward <= HOLD):
            start = arrived(*matmuls[0][:2])
        if ready and ready[0][0] <= now:
            pick = ready[0][1]
        elif start is not None and start <= now and not (ready and ready[0][0] < now + GAP_US):
            pick = ("matmul", *matmuls.pop(0))
        else:
            times = [when for when, _ in ready]
            if start is not None and start > now:
                times.append(start)
            if own and onward <= ONWARD:
                times.append(max(now, min(free[d] for _, d, _ in own) - QUEUE_US) + 0.01)
            now = min(times)
            continue
        ops.append(pick)
        kind, st, *rest = pick
        if kind == "ag":
            d, hop, q = rest
            del due[pick]
            now += GATHER_US
            held[st, slot_at(chips, d, hop), q] = now
            if hop < reach(chips, d, q):
                send(("ag", st, d, hop + 1, q), d)
                onward -= st == 0
        elif kind == "matmul":
            part, piece = rest
            if piece < tiles:
                now += GATE_UP_US
            else:
                now += DOWN_US
                scaled[st, part, (piece - tiles) // DOWNS] = now
        elif kind == "sum":
            d, hop, q = rest
            now += SUM_US
            sums.remove((st, d, hop, q))
            due.pop(("rs", st, d, hop + 1, q), None)
            send(("rs", st, d, hop, q), 1 - d)
        else:
            now += SUM_US
            closes.remove((st, *rest))
            for d in range(2):
                del due["rs", st, d, 1, *rest]
    return ops


def kernel(
    chips,
    across,
    hidden_ref,
    ids_hbm,
    weights_hbm,
    gate_hbm,
    up_hbm,
    down_hbm,
    out,
    ids_ref,
    weights_ref,
    gate_sum,
    x,
    pc,
    rs,
    table,
    gate,
    up,
    down,
    mid,
    scale,
    load_sem,
    ag_s,
    ag_r,
    pf_s,
    pf_r,
    pc_s,
    pc_r,
    rs_s,
    rs_r,
    tb_s,
    tb_r,
    tp_s,
    tp_r,
):
    steps, _, _, rows, width = x.shape
    inner = gate.shape[1]
    experts = 2 * chips
    along = chips // across

    me = lax.axis_index("expert")
    core = lax.rem(me, 2)
    chip = lax.div(me, 2)
    if across == 2:
        far, deep = lax.rem(chip, 2), lax.div(chip, 2)
        here = (1 - far) * deep + far * (2 * along - 1 - deep)
    else:
        here = chip

    def device_at(position):
        if across == 2:
            far = lax.div(position, along)
            deep = (1 - far) * position + far * (2 * along - 1 - position)
            position = deep * 2 + far
        return {"expert": position * 2 + core}

    sign = 1 - 2 * core
    neighbours = (
        device_at(lax.rem(here + sign + chips, chips)),
        device_at(lax.rem(here - sign + chips, chips)),
    )
    partner = {"expert": chip * 2 + (1 - core)}
    slot = functools.partial(slot_at, chips)
    order = slots_in_order(chips)
    place = {s: i for i, s in enumerate(order)}
    per = chips // PARTS
    part_of = {s: i // per for i, s in enumerate(order)}
    high, wide = rows // 2, width // SIDES

    def mirror(s):
        return (chips - s) % chips

    def area(q):
        return pl.ds(q // SIDES * high, high), pl.ds(q % SIDES * wide, wide)

    def remote(src, dst, send, recv, target):
        return pltpu.make_async_remote_copy(
            src_ref=src,
            dst_ref=dst,
            send_sem=send,
            recv_sem=recv,
            device_id=target,
            device_id_type=MESH,
        )

    def ag_copy(st, d, hop, q):
        return remote(
            x.at[st, place[slot(d, hop - 1)], 0, *area(q)],
            x.at[st, place[slot(d, hop)], 0, *area(q)],
            ag_s.at[st, part_of[slot(d, hop - 1)]],
            ag_r.at[st, place[slot(d, hop)] - 1, q],
            neighbours[d],
        )

    def pf_copy(st, s, q):
        return remote(
            x.at[st, place[s], 0, *area(q)],
            x.at[st, place[mirror(s)], 1, *area(q)],
            pf_s.at[st, part_of[s]],
            pf_r.at[st, part_of[mirror(s)]],
            partner,
        )

    def pc_copy(st, s, c):
        columns = pl.ds(c * wide, wide)
        return remote(
            x.at[st, place[s], 1, :, columns],
            pc.at[st, mirror(s), :, columns],
            pc_s,
            pc_r.at[st, part_of[s], c],
            partner,
        )

    def rs_copy(st, d, hop, q):
        target = slot(d, hop - 1) if (d == 0 or hop > 1) else chips // 2
        return remote(
            x.at[st, place[slot(d, hop)], 0, *area(q)],
            rs.at[st, target, *area(q)],
            rs_s,
            rs_r.at[st, target, q],
            neighbours[1 - d],
        )

    def tb_copy(d, hop):
        return remote(
            table.at[place[slot(d, hop - 1)], 0],
            table.at[place[slot(d, hop)], 0],
            tb_s,
            tb_r.at[place[slot(d, hop)] - 1],
            neighbours[d],
        )

    def tp_copy(s):
        return remote(
            table.at[place[s], 0],
            table.at[place[mirror(s)], 1],
            tp_s,
            tp_r.at[part_of[mirror(s)]],
            partner,
        )

    barrier = pltpu.get_barrier_semaphore()
    for target in (*neighbours, partner):
        pl.semaphore_signal(barrier, inc=1, device_id=target, device_id_type=MESH)

    own = [
        pltpu.make_async_copy(hidden_ref.at[st], x.at[st, 0, 0], load_sem.at[3 + st])
        for st in range(steps)
    ]
    for copy in own:
        copy.start()
    loads = [
        pltpu.make_async_copy(src.at[0], dst, load_sem.at[i])
        for i, (src, dst) in enumerate(((gate_hbm, gate), (up_hbm, up), (down_hbm, down)))
    ]
    small = [
        pltpu.make_async_copy(src, dst, load_sem.at[3 + steps + i])
        for i, (src, dst) in enumerate(((ids_hbm, ids_ref), (weights_hbm, weights_ref)))
    ]
    for copy in small:
        copy.start()
    for copy in loads:
        copy.start()
    pl.semaphore_wait(barrier, 3)

    listed, lanes = table.shape[2:]

    def table_open():
        for copy in small:
            copy.wait()
        label = lax.broadcasted_iota(jnp.int32, (experts, rows), 0)
        for st in range(steps):
            raw = weights_ref[st]
            normalized = raw / jnp.sum(raw, axis=0, keepdims=True)
            ids = ids_ref[st]
            dense = jnp.zeros((experts, rows), jnp.float32)
            for k in range(ids.shape[0]):
                dense = dense + jnp.where(label == ids[k : k + 1], normalized[k : k + 1], 0.0)
            for g in range(experts // listed):
                lane = (g * steps + st) * rows
                table[0, 0, :, pl.ds(lane, rows)] = dense[g * listed : (g + 1) * listed]
        for d in range(2):
            tb_copy(d, 1).start()
        tp_copy(0).start()

    def table_event(d, hop):
        tb_copy(d, hop).wait_recv()
        if hop < reach(chips, d, 0):
            tb_copy(d, hop + 1).start()
        tp_copy(slot(d, hop)).start()

    def ag_event(st, d, hop, q):
        if st == 0 and q == 1 and hop <= reach(chips, d, 0):
            table_event(d, hop)
        ag_copy(st, d, hop, q).wait_recv()
        if hop < reach(chips, d, q):
            ag_copy(st, d, hop + 1, q).start()
        pf_copy(st, slot(d, hop), q).start()

    summed = set()

    def partner_sums(st, s, c):
        key = (st, part_of[mirror(s)], c)
        if key not in summed:
            summed.add(key)
            some = pc.at[st, pl.ds(0, per), :, pl.ds(c * wide, wide)]
            pltpu.make_async_copy(some, some, pc_r.at[key]).wait()

    def total(st, s, received, q):
        partner_sums(st, s, q % SIDES)
        value = x[st, place[s], 0, *area(q)].astype(jnp.float32)
        value = value + pc[st, s, *area(q)].astype(jnp.float32)
        for index in received:
            value = value + rs[st, index, *area(q)].astype(jnp.float32)
        return value.astype(jnp.bfloat16)

    def rs_event(st, d, hop, q):
        s = slot(d, hop)
        received = []
        if hop < reach(chips, d, q):
            rs_copy(st, d, hop + 1, q).wait_recv()
            received = [s]
        x[st, place[s], 0, *area(q)] = total(st, s, received, q)
        rs_copy(st, d, hop, q).start()

    def rs_close(st, q):
        for d in range(2):
            rs_copy(st, d, 1, q).wait_recv()
        out[st, *area(q)] = total(st, 0, [0, chips // 2], q)

    block = min(4, per)
    tall = block * 2 * rows
    ff_tile = 256 if inner % 256 == 0 else inner
    tiles = 2 * inner // ff_tile

    def over_blocks(first, body):
        if per == block:
            body(first, 0)
        else:
            def step(i, carry):
                body(first + i * block, i * tall)
                return carry

            lax.fori_loop(0, per // block, step, 0)

    def gate_up(st, part, tile):
        columns = pl.ds(tile // 2 * ff_tile, ff_tile)

        def body(first, row):
            rows_in = x[st, pl.ds(first, block)].reshape(tall, width)
            if tile % 2 == 0:
                g = jnp.dot(rows_in, gate[:, columns], preferred_element_type=jnp.float32)
                gate_sum[pl.ds(row, tall)] = g / (1.0 + jnp.exp(-g))
            else:
                u = jnp.dot(rows_in, up[:, columns], preferred_element_type=jnp.float32)
                mid[pl.ds(row, tall), columns] = (gate_sum[pl.ds(row, tall)] * u).astype(jnp.bfloat16)

        over_blocks(part * per, body)

    def fill_scale(st, part):
        if st == 0:
            some = table.at[pl.ds(0, per), 0]
            pltpu.make_async_copy(some, some, tp_r.at[part]).wait()
        spot = lax.broadcasted_iota(jnp.int32, (listed, lanes), 0)
        mine, beside = lax.rem(me, listed), lax.div(me, listed)
        blocks = 2 * block
        column = lax.broadcasted_iota(jnp.int32, (tall, blocks), 1)
        group = lax.broadcasted_iota(jnp.int32, (tall, blocks), 0) // rows

        def body(first, row):
            picked = [
                jnp.sum(jnp.where(spot == mine, table[first + i, c], 0.0), axis=0, keepdims=True)
                for i in range(block)
                for c in range(2)
            ]
            turned = jnp.concatenate(picked, axis=0).T
            own_rows = sum(
                jnp.where(beside == g, turned[lane : lane + rows], 0.0)
                for g in range(experts // listed)
                for lane in ((g * steps + st) * rows,)
            )
            spread = jnp.concatenate([own_rows] * blocks, axis=0)
            weight = jnp.sum(jnp.where(column == group, spread, 0.0), axis=1, keepdims=True)
            scale[pl.ds(row, tall), :] = jnp.broadcast_to(weight, (tall, LANES))

        over_blocks(part * per, body)

    def down_part(st, part, piece):
        c, third = piece // DOWNS, piece % DOWNS
        if piece == 0:
            fill_scale(st, part)
            onward = sum(
                hop < reach(chips, d, q)
                for d in range(2)
                for q in range(2 * SIDES)
                for hop in range(reach(chips, d, q))
                if part_of[slot(d, hop)] == part
            )
            for blocks, sem in ((onward // (2 * SIDES), ag_s), (per, pf_s)):
                some = x.at[st, pl.ds(0, blocks), 0]
                pltpu.make_async_copy(some, some, sem.at[st, part]).wait()
        start, stop = (wide // LANES * (third + i) // DOWNS * LANES for i in range(2))
        columns = pl.ds(c * wide + start, stop - start)

        def body(first, row):
            v = jnp.dot(
                mid[pl.ds(row, tall), :], down[:, columns], preferred_element_type=jnp.float32
            )
            weight = scale[pl.ds(row, tall), :]
            v = v * jnp.concatenate([weight] * ((stop - start) // LANES), axis=1)
            v = v.astype(jnp.bfloat16).reshape(block, 2, rows, stop - start)
            x[st, pl.ds(first, block), :, :, columns] = v

        over_blocks(part * per, body)
        if third == DOWNS - 1:
            for s in order[part * per : (part + 1) * per]:
                pc_copy(st, s, c).start()

    arrived = set()
    loaded = set()

    def matmul_event(st, part, piece):
        if (st, part) not in arrived:
            arrived.add((st, part))
            some = x.at[st, pl.ds(0, per), 1]
            pltpu.make_async_copy(some, some, pf_r.at[st, part]).wait()
        if not loaded:
            loaded.add(0)
            for copy in loads:
                copy.wait()
        if piece < tiles:
            gate_up(st, part, piece)
        else:
            down_part(st, part, piece - tiles)

    begun = set()

    def own_event(st, d, q):
        if st not in begun:
            begun.add(st)
            own[st].wait()
        ag_copy(st, d, 1, q).start()
        if q == SIDES * 2 - 1 and d == 1:
            for c in range(2 * SIDES):
                pf_copy(st, 0, c).start()
            if st == 0:
                table_open()

    run = {
        "own": own_event,
        "ag": ag_event,
        "matmul": matmul_event,
        "sum": rs_event,
        "close": rs_close,
    }
    for name, *where in plan(chips, steps, tiles):
        run[name](*where)

    for sent, sem in (
        (x.at[:, :, 1], pc_s),
        (x.at[:, pl.ds(0, chips - 1), 0], rs_s),
        (table.at[pl.ds(0, chips - 1), 0], tb_s),
        (table.at[:, 0], tp_s),
    ):
        pltpu.make_async_copy(sent, sent, sem).wait()


def on_device(across, hidden_states, route_ids, route_weights, gate_proj, up_proj, down_proj):
    steps, rows, width = hidden_states.shape
    experts = lax.axis_size("expert")
    inner = gate_proj.shape[2]
    chips = experts // 2
    per = chips // PARTS
    beside = max(1, LANES // (steps * rows))
    beside = beside if experts % (8 * beside) == 0 else 1
    lanes = -(-steps * rows * beside // LANES) * LANES
    dma = pltpu.SemaphoreType.DMA
    bf16 = jnp.bfloat16
    hbm = pl.BlockSpec(memory_space=pl.ANY)
    return pl.pallas_call(
        functools.partial(kernel, chips, across),
        out_shape=pltpu.VMEM((steps, rows, width), bf16),
        in_specs=[hbm] * 6,
        out_specs=pl.BlockSpec(memory_space=pltpu.VMEM),
        scratch_shapes=[
            pltpu.VMEM((steps, route_ids.shape[2], rows), jnp.int32),
            pltpu.VMEM((steps, route_ids.shape[2], rows), jnp.float32),
            pltpu.VMEM((per * 2 * rows, 256 if inner % 256 == 0 else inner), jnp.float32),
            pltpu.VMEM((steps, chips, 2, rows, width), bf16),
            pltpu.VMEM((steps, chips, rows, width), bf16),
            pltpu.VMEM((steps, chips, rows, width), bf16),
            pltpu.VMEM((chips, 2, experts // beside, lanes), jnp.float32),
            pltpu.VMEM((width, inner), bf16),
            pltpu.VMEM((width, inner), bf16),
            pltpu.VMEM((inner, width), bf16),
            pltpu.VMEM((per * 2 * rows, inner), bf16),
            pltpu.VMEM((per * 2 * rows, LANES), jnp.float32),
            dma((5 + steps,)),
            dma((steps, PARTS)),
            dma((steps, chips - 1, 2 * SIDES)),
            dma((steps, PARTS)),
            dma((steps, PARTS)),
            dma,
            dma((steps, PARTS, SIDES)),
            dma,
            dma((steps, chips, 2 * SIDES)),
            dma,
            dma((chips - 1,)),
            dma,
            dma((PARTS,)),
        ],
        compiler_params=pltpu.CompilerParams(
            collective_id=0, has_side_effects=True, vmem_limit_bytes=64_000_000
        ),
    )(hidden_states, route_ids.swapaxes(1, 2), route_weights.swapaxes(1, 2), gate_proj, up_proj, down_proj)


def solution(mesh):
    across = 2 if mesh.shape["groups"] == 2 else 1
    placed = (
        P(None, ("groups", "expert"), None),
        P(None, ("groups", "expert"), None),
        P(None, ("groups", "expert"), None),
        P("expert", None, None),
        P("expert", None, None),
        P("expert", None, None),
    )
    return jax.shard_map(
        functools.partial(on_device, across),
        mesh=mesh,
        in_specs=placed,
        out_specs=P(None, ("groups", "expert"), None),
        check_vma=False,
    )
```
